256 devices in a mesh: dp: 32 (over z, y_lo, core), mp: 8 (over y_hi, x).
Axes of the slice: x: 4, y: 4 (y_hi: 2, y_lo: 2; y = y_hi * 2 + y_lo), z: 8, core: 2. Of those that a mesh axis runs over, the one named last changes fastest.
Arguments:
- upper_first: bfloat16 [8192, 4096], P('dp'), may hold values from -6 to 6
- upper_second: bfloat16 [8192, 4096], P('dp'), may hold values from -24 to 24
- grad_first: bfloat16 [8192, 4096], P('dp'), may hold values from -6 to 6
- grad_second: bfloat16 [8192, 4096], P('dp'), may hold values from -6 to 6
- norm_gain: bfloat16 [4096], replicated, may hold values from 0.25 to 1.75
- up_weight: bfloat16 [4096, 11264], P('dp', 'mp'), may hold values from -0.09375 to 0.09375
- down_weight: bfloat16 [4096, 11264], P('dp', 'mp'), may hold values from -0.0546875 to 0.0546875
- adapter_down: bfloat16 [4096, 64], replicated, may hold values from -0.09375 to 0.09375
- adapter_up: bfloat16 [64, 4096], replicated, may hold values from -0.75 to 0.75
Outputs:
- lower_first: bfloat16 [8192, 4096], P('dp', 'mp')
- lower_second: bfloat16 [8192, 4096], P('dp', 'mp')
- input_grad_first: bfloat16 [8192, 4096], P('dp', 'mp')
- input_grad_second: bfloat16 [8192, 4096], P('dp')
- adapter_down_grad: float32 [4096, 64], P('mp')
- adapter_up_grad: float32 [64, 4096], P(None, 'mp')
The draws below stay inside these ranges and needn't reach their ends.
All inputs are finite; a program needn't handle non-finite values.
Results may differ from the reference program's by a relative error of at most 0.009.
Values may be sent and summed in bfloat16 or wider, within the bound.
A program may use at most 128 MiB of HBM per device.

```python
import math
import jax
import jax.numpy as jnp
from jax import lax

D = 4096
FF = 11264
R = 64
TOKENS = 8192
N_MP = 8


def draw_upper_second(key, part):
    first_key, second_key = jax.random.split(jax.random.fold_in(key, 71), 2)
    base = jax.random.normal(first_key, (TOKENS, D), jnp.float32)
    row_scales = jnp.exp(jax.random.uniform(second_key, (TOKENS, 1), jnp.float32, math.log(0.6), math.log(6.0)))
    values = base * row_scales
    return jnp.clip(values, -24.0, 24.0).astype(jnp.bfloat16)


def steps_of(key, shape, pieces, least, high):
    factor_of, own = 1.0, jax.random.fold_in(key, 6)
    for axis_at, parts in pieces:
        heights = jnp.exp(jax.random.uniform(jax.random.fold_in(own, axis_at), (parts,), jnp.float32, least / len(pieces), high / len(pieces)))
        factor_of = factor_of * jnp.repeat(heights, shape[axis_at] // parts).reshape([-1 if axis == axis_at else 1 for axis in range(len(shape))])
    return factor_of


def centred(rng, shape, spread, limit, cuts=(), dtype=jnp.bfloat16):
    drawn = spread * jax.random.normal(rng, shape, jnp.float32)
    if cuts:
        drawn = drawn * steps_of(rng, shape, cuts, -0.22, 0.18)
    return jnp.clip(drawn, -limit, limit).astype(dtype)


def setup_inputs(seed: int = 0) -> dict:
    seeds = jax.random.split(jax.random.key(seed), 10)
    upper_first = centred(seeds[0], (TOKENS, D), 1.0, 6.0, ((0, 32),))
    upper_second = draw_upper_second(jax.random.fold_in(seeds[9], 71), 0)
    grad_first = centred(seeds[2], (TOKENS, D), 1.0, 6.0, ((0, 32),))
    grad_second = centred(seeds[3], (TOKENS, D), 1.0, 6.0, ((0, 32),))
    norm_gain = jnp.clip(1.0 + 0.15 * jax.random.normal(seeds[4], (D,), jnp.float32), 0.25, 1.75).astype(jnp.bfloat16)
    up_weight = centred(seeds[5], (D, FF), D ** -0.5, 0.09375, ((0, 32), (1, 8)))
    down_weight = centred(seeds[6], (D, FF), FF ** -0.5, 0.0546875, ((0, 32), (1, 8)))
    adapter_down = centred(seeds[7], (D, R), D ** -0.5, 0.09375)
    adapter_up = centred(seeds[8], (R, D), R ** -0.5, 0.75)
    return {"upper_first": upper_first, "upper_second": upper_second, "grad_first": grad_first, "grad_second": grad_second, "norm_gain": norm_gain, "up_weight": up_weight, "down_weight": down_weight, "adapter_down": adapter_down, "adapter_up": adapter_up}


def silu_slope(argument):
    sigmoid_value = jax.nn.sigmoid(argument)
    return sigmoid_value * (1.0 + argument * (1.0 - sigmoid_value))

def reference(upper_first, upper_second, grad_first, grad_second, norm_gain, up_weight, down_weight, adapter_down, adapter_up):
    pre_adapter = jnp.dot(upper_first, adapter_down, preferred_element_type=jnp.float32)
    squashed = jax.nn.silu(pre_adapter).astype(jnp.bfloat16)
    adapted = jnp.dot(squashed, adapter_up, preferred_element_type=jnp.float32)
    lower_second = (upper_second.astype(jnp.float32) - adapted).astype(jnp.bfloat16)
    lower_value = lower_second.astype(jnp.float32)
    inverse_rms = lax.rsqrt(lax.optimization_barrier(jnp.mean(lower_value * lower_value, axis=1, keepdims=True)) + 1e-05)
    gain_full = norm_gain.astype(jnp.float32)
    normed = (lower_value * inverse_rms * gain_full).astype(jnp.bfloat16)
    hidden_pre = jnp.dot(normed, up_weight, preferred_element_type=jnp.float32)
    activated = jax.nn.silu(hidden_pre).astype(jnp.bfloat16)
    block_width = FF // N_MP
    frozen_out = jnp.zeros((TOKENS, D), jnp.float32)
    for block in range(N_MP):
        lo_col = block * block_width
        partial_out = jnp.dot(activated[:, lo_col:lo_col + block_width], down_weight[:, lo_col:lo_col + block_width].T, preferred_element_type=jnp.float32)
        rounded = lax.optimization_barrier(partial_out.astype(jnp.bfloat16))
        frozen_out = frozen_out + rounded.astype(jnp.float32)
    lower_first = ((upper_first.astype(jnp.float32) - frozen_out) / 0.5).astype(jnp.bfloat16)
    adapter_slope = jnp.dot(grad_second, adapter_up.T, preferred_element_type=jnp.float32)
    adapter_pre_grad = (adapter_slope * silu_slope(pre_adapter)).astype(jnp.bfloat16)
    carried = (grad_first.astype(jnp.float32) + jnp.dot(adapter_pre_grad, adapter_down.T, preferred_element_type=jnp.float32)).astype(jnp.bfloat16)
    input_grad_first = (0.5 * carried.astype(jnp.float32)).astype(jnp.bfloat16)
    grad_scale = 1.0 / jnp.sqrt(jnp.float32(TOKENS))
    adapter_down_grad = jnp.dot(upper_first.T, adapter_pre_grad, preferred_element_type=jnp.float32) * grad_scale
    adapter_up_grad = jnp.dot(squashed.T, grad_second, preferred_element_type=jnp.float32) * grad_scale
    act_grad = jnp.dot(carried, down_weight, preferred_element_type=jnp.float32)
    pre_grad = (act_grad * silu_slope(hidden_pre)).astype(jnp.bfloat16)
    normed_grad = jnp.dot(pre_grad, up_weight.T, preferred_element_type=jnp.float32)
    curvature = lax.optimization_barrier(jnp.sum(hidden_pre * pre_grad.astype(jnp.float32), axis=1, keepdims=True))
    input_grad_second = (grad_second.astype(jnp.float32) + inverse_rms * gain_full * normed_grad - lower_value * inverse_rms * inverse_rms * curvature / D).astype(jnp.bfloat16)
    return (lower_first, lower_second, input_grad_first, input_grad_second, adapter_down_grad, adapter_up_grad)
```

```python
import functools
import math

import jax
import jax.numpy as jnp
from jax import lax
from jax.experimental import pallas as pl
from jax.experimental.pallas import tpu as pltpu
from jax.sharding import PartitionSpec as P

MESH = pl.DeviceIdType.MESH
D = 4096
H = 1408
T = 256
R = 64
NZ = 8
NM = 8
UNIT = 64
CARRY = 3
GROUP = 256
LAYER = 512
CHUNKS = D // GROUP
HCUTS = ((0, 512), (512, 512), (1024, 384))
SHARE = T // NM
F32 = jnp.float32
BF16 = jnp.bfloat16
GRAD_SCALE = 1.0 / math.sqrt(8192.0)


def dot(a, b):
    return jnp.dot(a, b, preferred_element_type=F32)


def dot_nt(a, b):
    return lax.dot_general(a, b, (((1,), (1,)), ((), ())), preferred_element_type=F32)


def sigmoid(v):
    return 1.0 / (1.0 + jnp.exp(-v))


def wait_bytes(ref, sem):
    pltpu.make_async_copy(ref, ref, sem).wait()


def kernel(
    uf_hbm, us_hbm, gf_hbm, gs_hbm, gain_ref, upw, dnw, adt_hbm, au_hbm,
    o_lf, o_ls, o_igf, o_igs, o_dg, o_ug,
    uf, us, gf, gs, norm, adt, au,
    up, dn, hp, ag, slope, act, pg,
    fs, fr, ns, nr, outc,
    pre, sl, ssq, invb, curv, stat, sr,
    grad, gr1, gr2, gr3, gfin,
    in_sem, ad_sem, init_sem, isend, zrecv, zsend, yrecv, ysend, srecv, ssend,
    fsend, frecv, nsend, nrecv, tsend, trecv, gsend, grecv, osend, orecv, osem,
):
    dp = lax.axis_index("dp")
    m = lax.axis_index("mp")
    c = lax.rem(dp, 2)
    y = lax.rem(dp // 2, 2)
    z = dp // 4
    home = jnp.where(y == c, 1, 0)

    def dev(z_, y_, c_, m_):
        return ((z_ * 2 + y_) * 2 + c_, m_)

    sib = dev(z, y, 1 - c, m)
    ypal = dev(z, 1 - y, c, m)
    step_z = jnp.where(c == 0, 1, NZ - 1)
    znext = dev(lax.rem(z + step_z, NZ), y, c, m)
    zshift = [lax.rem(z + k, NZ) for k in range(NZ)]
    mshift = [lax.rem(m + k, NM) for k in range(NM)]
    zdev = [dev(zshift[k], y, c, m) for k in range(NZ)]
    mdev = [dev(z, y, c, mshift[k]) for k in range(NM)]

    def send(src, dst, ssem, rsem, to):
        pltpu.make_async_remote_copy(
            src_ref=src, dst_ref=dst, send_sem=ssem, recv_sem=rsem, device_id=to, device_id_type=MESH
        ).start()

    barrier = pltpu.get_barrier_semaphore()
    partners = [zdev[k] for k in range(1, NZ)] + [dev(z, 1 - y, 0, m), dev(z, 1 - y, 1, m), sib]
    partners += [mdev[k] for k in range(1, NM)]
    for p in partners:
        pl.semaphore_signal(barrier, inc=1, device_id=p, device_id_type=MESH)
    pl.semaphore_wait(barrier, len(partners))

    weights = ((upw, up), (dnw, dn))
    first = z * LAYER + y * GROUP + c * 128
    for w, (src, dst) in enumerate(weights):
        for h in range(2):
            rows = pl.ds(pl.multiple_of(first + h * UNIT, UNIT), UNIT)
            piece = src.at[pl.ds(h * UNIT, UNIT)]
            send(piece, dst.at[rows], isend.at[w, 0], init_sem.at[w, 2 * c + h], dev(z, 1 - y, y, m))

            @pl.when(home == 1)
            def _():
                pltpu.make_async_copy(piece, dst.at[rows], init_sem.at[w, 2 * c + h]).start()

            @pl.when(home == 0)
            def _():
                send(piece, dst.at[rows], isend.at[w, 1], init_sem.at[w, 2 * c + h], sib)

    ins = ((uf_hbm, uf), (gs_hbm, gs), (us_hbm, us), (gf_hbm, gf))
    for src, dst in ((adt_hbm, adt), (au_hbm, au)):
        for k in range(CHUNKS):
            pltpu.make_async_copy(src.at[:, pl.ds(k * GROUP, GROUP)], dst.at[k], ad_sem).start()
    for i, (src, dst) in enumerate(ins):
        for k in range(CHUNKS):
            pltpu.make_async_copy(src.at[:, pl.ds(k * GROUP, GROUP)], dst.at[k], in_sem.at[i]).start()

    def own_layer(s):
        return lax.rem(jnp.where(c == 0, z + NZ - s, z + s), NZ)

    def sib_layer(s):
        return lax.rem(jnp.where(c == 0, z + s, z + NZ - s), NZ)

    def rows_at(layer, group, offset, count):
        return pl.ds(pl.multiple_of(layer * LAYER + group * GROUP + offset, UNIT), count)

    def poll(w, s):
        first_step = isinstance(s, int) and s == 0
        buf = weights[w][1]
        layer = own_layer(s)
        for j in range(CARRY):
            region = buf.at[rows_at(layer, c, UNIT * home + UNIT * j, UNIT)]
            wait_bytes(region, init_sem.at[w, j + home] if first_step else zrecv.at[w, s, j])

            @pl.when(s < NZ - 1)
            def _():
                send(region, region, zsend.at[w], zrecv.at[w, s + 1, j], znext)

        if not first_step:
            region = buf.at[rows_at(layer, c, 3 * UNIT * home, UNIT)]
            send(region, region, ysend.at[w], yrecv.at[w, s], ypal)

    def late(w, s):
        first_step = isinstance(s, int) and s == 0
        buf = weights[w][1]
        layer = own_layer(s)
        region = buf.at[rows_at(layer, c, 3 * UNIT * (1 - home), UNIT)]
        wait_bytes(region, init_sem.at[w, 3 * (1 - home)] if first_step else yrecv.at[w, s])
        region = buf.at[rows_at(layer, c, 0, GROUP)]
        send(region, region, ssend.at[w], srecv.at[w, s], sib)

    def ready(w, s):
        wait_bytes(weights[w][1].at[rows_at(sib_layer(s), 1 - c, 0, GROUP)], srecv.at[w, s])

    def product_step(w, s, left, acc):
        buf = weights[w][1]
        own, other = own_layer(s), sib_layer(s)
        own_rows, other_rows = rows_at(own, c, 0, GROUP), rows_at(other, 1 - c, 0, GROUP)
        a, b = left[own * 2 + c], left[other * 2 + 1 - c]
        for lo, n in HCUTS:
            acc[:, lo:lo + n] += dot(a, buf[own_rows, lo:lo + n]) + dot(b, buf[other_rows, lo:lo + n])

    def hidden_step(s):
        ready(0, s)
        product_step(0, s, norm, hp)

    def frozen_block(layer, group):
        k = layer * 2 + group
        fs[k] = dot_nt(act[...], dn[rows_at(layer, group, 0, GROUP), :]).astype(BF16)
        shift = lax.rem(layer + NM - m, NM)

        @pl.when(shift != 0)
        def _():
            send(fs.at[k], fr.at[shift - 1, group], fsend, frecv, (dp, layer))

    def down_step(s):
        ready(1, s)
        product_step(1, s, gf, ag)
        frozen_block(own_layer(s), c)
        frozen_block(sib_layer(s), 1 - c)

    def adapter_in():
        wait_bytes(adt, ad_sem)
        wait_bytes(au, ad_sem)
        wait_bytes(uf, in_sem.at[0])
        wait_bytes(gs, in_sem.at[1])
        pre[...] = jnp.zeros_like(pre)
        sl[...] = jnp.zeros_like(sl)

        def body(k, _):
            pre[...] += dot_nt(uf[k], adt[k])
            sl[...] += dot_nt(gs[k], au[k])
            return 0

        lax.fori_loop(0, CHUNKS, body, 0)
        v = pre[...]
        s = sigmoid(v)
        pre[...] = v * s
        sl[...] = sl[...] * (s * (1.0 + v * (1.0 - s)))
        wait_bytes(us, in_sem.at[2])
        wait_bytes(gf, in_sem.at[3])
        ssq[...] = jnp.zeros_like(ssq)

    def adapter_out(lo, hi):
        squashed = pre[...].astype(BF16)
        slope_in = sl[...].astype(BF16)

        def body(k, _):
            lower = (us[k].astype(F32) - dot(squashed, au[k])).astype(BF16)
            us[k] = lower
            value = lower.astype(F32)
            square = value * value
            ssq[...] += square[:, :128] + square[:, 128:]
            gf[k] = (gf[k].astype(F32) + dot(slope_in, adt[k])).astype(BF16)
            return 0

        lax.fori_loop(lo, hi, body, 0)

    def normalise():
        mean = jnp.sum(ssq[...], axis=1, keepdims=True) * (1.0 / D)
        invb[...] = jnp.broadcast_to(lax.rsqrt(mean + 1e-05), (T, 128))

        def body(k, _):
            scale = invb[...]
            both = jnp.concatenate([scale, scale], axis=1)
            norm[k] = (us[k].astype(F32) * both * gain_ref[k]).astype(BF16)
            return 0

        lax.fori_loop(0, CHUNKS, body, 0)
        hp[...] = jnp.zeros_like(hp)
        ag[...] = jnp.zeros_like(ag)

    def grads_1():
        both = jnp.concatenate([sl[...], pre[...]], axis=1)
        turned = both.T.astype(BF16)
        for half, (rows, right) in enumerate(((turned[:R], uf), (turned[R:], gs))):
            for q in range(2):
                part = dot(rows, right[2 * m + q])
                for yy in range(2):
                    for t in range(4):
                        lo = yy * 32 + t * 8
                        grad[half, yy, 2 * t + q] = part[lo:lo + 8]
        send(grad.at[1 - c], gr1, gsend.at[0], grecv.at[0], sib)

    def grads_2():
        wait_bytes(gr1, grecv.at[0])
        grad[c] = grad[c] + gr1[...]
        send(grad.at[c, 1 - y], gr2, gsend.at[1], grecv.at[1], ypal)

    def grads_3():
        wait_bytes(gr2, grecv.at[1])
        grad[c, y] = grad[c, y] + gr2[...]
        for k in range(1, NZ):
            send(grad.at[c, y, zshift[k]], gr3.at[k - 1], gsend.at[2], grecv.at[2], zdev[k])

    def grads_4():
        wait_bytes(gr3, grecv.at[2])
        total = grad[c, y, z]
        for k in range(NZ - 1):
            total = total + gr3[k]
        gfin[c, y, z] = total * GRAD_SCALE
        for k in range(1, NZ):
            send(gfin.at[c, y, z], gfin.at[c, y, z], gsend.at[3], grecv.at[3], zdev[k])

    def grads_5():
        wait_bytes(gr3, grecv.at[3])
        send(gfin.at[c, y], gfin.at[c, y], gsend.at[4], grecv.at[4], ypal)

    def grads_6():
        wait_bytes(gr2, grecv.at[4])
        send(gfin.at[c], gfin.at[c], gsend.at[5], grecv.at[5], sib)

    def grads_7():
        wait_bytes(gr1, grecv.at[5])
        for half, out in enumerate((o_dg, o_ug)):
            for yy in range(2):
                for t in range(4):
                    for q in range(2):
                        lo = yy * 32 + t * 8
                        out[lo:lo + 8, q * 256:q * 256 + 256] = gfin[half, yy, 2 * t + q]

    def activations():
        def body(i, _):
            rows = pl.ds(pl.multiple_of(i * 32, 32), 32)
            v = hp[rows, :]
            s = sigmoid(v)
            act[rows, :] = (v * s).astype(BF16)
            slope[rows, :] = s * (1.0 + v * (1.0 - s))
            return 0

        lax.fori_loop(0, 8, body, 0)

    def slices_out():
        for q in range(2):
            lo = q * 256
            o_ls[:, lo:lo + 256] = us[2 * m + q]
            o_igf[:, lo:lo + 256] = (0.5 * gf[2 * m + q].astype(F32)).astype(BF16)

    poll(0, 0)
    adapter_in()
    late(0, 0)
    poll(0, 1)
    adapter_out(0, CHUNKS // 2)
    late(0, 1)
    poll(0, 2)
    adapter_out(CHUNKS // 2, CHUNKS)
    late(0, 2)
    normalise()

    def up_body(s, _):
        poll(0, s)
        late(0, s - 1)

        @pl.when(s == 4)
        def _():
            grads_1()

        @pl.when(s == 5)
        def _():
            grads_2()

        @pl.when(s == 6)
        def _():
            grads_3()

        hidden_step(s - 3)
        return 0

    late_done = 3
    poll(0, 3)
    hidden_step(0)
    lax.fori_loop(late_done + 1, NZ, up_body, 0)
    poll(1, 0)
    hidden_step(5)
    late(0, 7)
    hidden_step(6)
    late(1, 0)
    poll(1, 1)
    hidden_step(7)
    activations()

    def down_body(s, _):
        poll(1, s)
        late(1, s - 1)

        @pl.when(s == 2)
        def _():
            grads_4()

        @pl.when(s == 3)
        def _():
            grads_5()

        @pl.when(s == 4)
        def _():
            grads_6()

        @pl.when(s == 5)
        def _():
            grads_7()
            slices_out()

        down_step(s - 2)
        return 0

    lax.fori_loop(2, NZ, down_body, 0)
    late(1, 7)
    down_step(6)
    down_step(7)

    def pre_grads(i, _):
        rows = pl.ds(pl.multiple_of(i * 32, 32), 32)
        g = (ag[rows, :] * slope[rows, :]).astype(BF16)
        pg[rows, :] = g
        part = jnp.sum(hp[rows, :] * g.astype(F32), axis=1, keepdims=True)
        stat[rows, :] = jnp.broadcast_to(part, (32, 128))
        return 0

    lax.fori_loop(0, 8, pre_grads, 0)
    mine = pl.ds(pl.multiple_of(m * SHARE, SHARE), SHARE)
    for k in range(1, NM):
        theirs = pl.ds(pl.multiple_of(mshift[k] * SHARE, SHARE), SHARE)
        send(stat.at[theirs], sr.at[k - 1], tsend, trecv, mdev[k])

    def normed_block(b, _):
        for q in range(2):
            rows = pl.ds(pl.multiple_of(b * LAYER + q * GROUP, GROUP), GROUP)
            ns[b, :, q * GROUP:q * GROUP + GROUP] = dot_nt(pg[...], up[rows, :]).astype(BF16)
        for k in range(1, NM):
            theirs = pl.ds(pl.multiple_of(mshift[k] * SHARE, SHARE), SHARE)
            send(ns.at[b, theirs], nr.at[b, k - 1], nsend, nrecv.at[b], mdev[k])
        return 0

    lax.fori_loop(0, NZ, normed_block, 0)

    wait_bytes(fr, frecv)
    for q in range(2):
        def rebuild(i, _):
            rows = pl.ds(pl.multiple_of(i * 32, 32), 32)
            total = fs[2 * m + q, rows, :].astype(F32)
            for k in range(NM - 1):
                total = total + fr[k, q, rows, :].astype(F32)
            o_lf[rows, q * GROUP:q * GROUP + GROUP] = (
                (uf[2 * m + q, rows, :].astype(F32) - total) * 2.0
            ).astype(BF16)
            return 0

        lax.fori_loop(0, 8, rebuild, 0)

    wait_bytes(sr, trecv)
    inv32 = invb[mine, :]
    total = stat[mine, :]
    for k in range(NM - 1):
        total = total + sr[k]
    curv[...] = inv32 * inv32 * total * (1.0 / D)

    def finish(b, _):
        wait_bytes(nr.at[b], nrecv.at[b])
        inv = invb[mine, :]
        inv = jnp.concatenate([inv, inv], axis=1)
        cv = jnp.concatenate([curv[...], curv[...]], axis=1)
        for q in range(2):
            lo = q * GROUP
            k2 = 2 * b + q
            normed_grad = ns[b, mine, lo:lo + GROUP].astype(F32)
            for k in range(NM - 1):
                normed_grad = normed_grad + nr[b, k, :, lo:lo + GROUP].astype(F32)
            outc[b, :, lo:lo + GROUP] = (
                gs[k2, mine, :].astype(F32)
                + inv * gain_ref[k2] * normed_grad
                - us[k2, mine, :].astype(F32) * cv
            ).astype(BF16)
        place = o_igs.at[mine, pl.ds(pl.multiple_of(b * LAYER, LAYER), LAYER)]
        for k in range(1, NM):
            send(outc.at[b], place, osend, orecv, mdev[k])
        pltpu.make_async_copy(outc.at[b], place, osem).start()
        return 0

    lax.fori_loop(0, NZ, finish, 0)

    seven = ns.at[:, pl.ds(0, T - SHARE)]
    for w in range(2):
        buf = weights[w][1]
        wait_bytes(buf.at[pl.ds(0, 2 * UNIT)], isend.at[w, 0])

        @pl.when(home == 0)
        def _():
            wait_bytes(buf.at[pl.ds(0, 2 * UNIT)], isend.at[w, 1])

        wait_bytes(buf.at[pl.ds(0, 7 * CARRY * UNIT)], zsend.at[w])
        wait_bytes(buf.at[pl.ds(0, 7 * UNIT)], ysend.at[w])
        wait_bytes(buf.at[pl.ds(0, 8 * GROUP)], ssend.at[w])
    wait_bytes(fr, fsend)
    wait_bytes(sr, tsend)
    wait_bytes(gr1, gsend.at[0])
    wait_bytes(gr2, gsend.at[1])
    wait_bytes(gr3, gsend.at[2])
    wait_bytes(gr3, gsend.at[3])
    wait_bytes(gr2, gsend.at[4])
    wait_bytes(gr1, gsend.at[5])
    wait_bytes(seven, nsend)
    wait_bytes(seven, osend)
    wait_bytes(outc, osem)
    wait_bytes(seven, orecv)


def on_device(uf, us, gf, gs, gain, upw, dnw, ad, au):
    any_spec = pl.BlockSpec(memory_space=pl.ANY)
    vmem = pl.BlockSpec(memory_space=pltpu.VMEM)
    sds = jax.ShapeDtypeStruct
    gain3 = gain.astype(F32).reshape(CHUNKS, 1, GROUP)
    dma = pltpu.SemaphoreType.DMA
    chunked = pltpu.VMEM((CHUNKS, T, GROUP), BF16)
    outs = pl.pallas_call(
        kernel,
        out_shape=(
            sds((T, 512), BF16), sds((T, 512), BF16), sds((T, 512), BF16), sds((T, D), BF16),
            sds((R, 512), F32), sds((R, 512), F32),
        ),
        in_specs=[any_spec] * 4 + [vmem] + [any_spec] * 4,
        out_specs=(vmem, vmem, vmem, any_spec, vmem, vmem),
        scratch_shapes=[
            chunked, chunked, chunked, chunked, chunked,
            pltpu.VMEM((CHUNKS, R, GROUP), BF16), pltpu.VMEM((CHUNKS, R, GROUP), BF16),
            pltpu.VMEM((D, H), BF16), pltpu.VMEM((D, H), BF16),
            pltpu.VMEM((T, H), F32), pltpu.VMEM((T, H), F32), pltpu.VMEM((T, H), F32),
            pltpu.VMEM((T, H), BF16), pltpu.VMEM((T, H), BF16),
            chunked, pltpu.VMEM((NM - 1, 2, T, GROUP), BF16),
            pltpu.VMEM((NZ, T, LAYER), BF16), pltpu.VMEM((NZ, NM - 1, SHARE, LAYER), BF16),
            pltpu.VMEM((NZ, SHARE, LAYER), BF16),
            pltpu.VMEM((T, R), F32), pltpu.VMEM((T, R), F32), pltpu.VMEM((T, 128), F32),
            pltpu.VMEM((T, 128), F32), pltpu.VMEM((SHARE, 128), F32), pltpu.VMEM((T, 128), F32),
            pltpu.VMEM((NM - 1, SHARE, 128), F32),
            pltpu.VMEM((2, 2, 8, 8, 256), F32), pltpu.VMEM((2, 8, 8, 256), F32),
            pltpu.VMEM((8, 8, 256), F32), pltpu.VMEM((7, 8, 256), F32),
            pltpu.VMEM((2, 2, 8, 8, 256), F32),
            dma((4,)), dma, dma((2, 4)), dma((2, 2)), dma((2, 8, 3)), dma((2,)), dma((2, 8)), dma((2,)),
            dma((2, 8)), dma((2,)),
            dma, dma, dma, dma((8,)), dma, dma, dma((6,)), dma((6,)), dma, dma, dma,
        ],
        compiler_params=pltpu.CompilerParams(
            collective_id=0, has_side_effects=True, vmem_limit_bytes=67000000
        ),
        name="coupling",
    )(uf, us, gf, gs, gain3, upw, dnw, ad.T, au)
    lf, ls, igf, igs, dgt, ug = outs
    return lf, ls, igf, igs, dgt.T, ug


def solution(mesh):
    return jax.shard_map(
        on_device,
        mesh=mesh,
        in_specs=(
            P("dp", None), P("dp", None), P("dp", None), P("dp", None), P(),
            P("dp", "mp"), P("dp", "mp"), P(), P(),
        ),
        out_specs=(
            P("dp", "mp"), P("dp", "mp"), P("dp", "mp"), P("dp", None), P("mp", None), P(None, "mp"),
        ),
        check_vma=False,
    )
```

```python
import functools
import math

import jax
import jax.numpy as jnp
from jax import lax
from jax.experimental import pallas as pl
from jax.experimental.pallas import tpu as pltpu
from jax.sharding import PartitionSpec as P

MESH = pl.DeviceIdType.MESH
D = 4096
H = 1408
T = 256
R = 64
NZ = 8
NM = 8
UNIT = 64
CARRY = 3
GROUP = 256
LAYER = 512
CHUNKS = D // GROUP
HCUTS = ((0, 512), (512, 512), (1024, 384))
SHARE = T // NM
F32 = jnp.float32
BF16 = jnp.bfloat16
GRAD_SCALE = 1.0 / math.sqrt(8192.0)


def dot(a, b):
    return jnp.dot(a, b, preferred_element_type=F32)


def dot_nt(a, b):
    return lax.dot_general(a, b, (((1,), (1,)), ((), ())), preferred_element_type=F32)


def sigmoid(v):
    return 1.0 / (1.0 + jnp.exp(-v))


def wait_bytes(ref, sem):
    pltpu.make_async_copy(ref, ref, sem).wait()


def kernel(
    uf_hbm, us_hbm, gf_hbm, gs_hbm, gain_ref, upw, dnw, adt_hbm, au_hbm,
    o_lf, o_ls, o_igf, o_igs, o_dg, o_ug,
    uf, us, gf, gs, norm, adt, au,
    up, dn, hp, ag, slope, act, pg,
    fs, fr, f2s, fr2, ns, nr, outc,
    pre, sl, ssq, invb, curv, stat, sr,
    grad, gr1, gr2, gr3, gfin,
    in_sem, ad_sem, yfirst, lsem, zrecv, zsend, yrecv, ysend, srecv, ssend,
    fsend, frecv, f2sem, nsend, nrecv, tsend, trecv, gsend, grecv, osend, orecv, osem,
):
    dp = lax.axis_index("dp")
    m = lax.axis_index("mp")
    c = lax.rem(dp, 2)
    y = lax.rem(dp // 2, 2)
    z = dp // 4
    x = lax.rem(m, 4)
    row_m = m - x

    def dev(z_, y_, c_, m_):
        return ((z_ * 2 + y_) * 2 + c_, m_)

    sib = dev(z, y, 1 - c, m)
    ypal = dev(z, 1 - y, c, m)
    step_z = jnp.where(c == 0, 1, NZ - 1)
    znext = dev(lax.rem(z + step_z, NZ), y, c, m)
    zshift = [lax.rem(z + k, NZ) for k in range(NZ)]
    mshift = [lax.rem(m + k, NM) for k in range(NM)]
    zdev = [dev(zshift[k], y, c, m) for k in range(NZ)]
    mdev = [dev(z, y, c, mshift[k]) for k in range(NM)]

    def send(src, dst, ssem, rsem, to):
        pltpu.make_async_remote_copy(
            src_ref=src, dst_ref=dst, send_sem=ssem, recv_sem=rsem, device_id=to, device_id_type=MESH
        ).start()

    barrier = pltpu.get_barrier_semaphore()
    partners = [zdev[k] for k in range(1, NZ)] + [dev(z, 1 - y, 0, m), dev(z, 1 - y, 1, m), sib]
    partners += [mdev[k] for k in range(1, NM)]
    for p in partners:
        pl.semaphore_signal(barrier, inc=1, device_id=p, device_id_type=MESH)
    pl.semaphore_wait(barrier, len(partners))

    weights = ((upw, up), (dnw, dn))
    mine_row = z * LAYER + c * GROUP + y * 128

    def first_y(w):
        src, buf = weights[w]
        for h, sem in ((0, yfirst.at[w]), (1, yrecv.at[w, 0])):
            dst = buf.at[pl.ds(pl.multiple_of(mine_row + h * UNIT, UNIT), UNIT)]
            send(src.at[pl.ds(h * UNIT, UNIT)], dst, ysend.at[w], sem, ypal)

    def first_z(w):
        src, buf = weights[w]
        for j, h in ((0, 1), (1, 0)):
            dst = buf.at[pl.ds(pl.multiple_of(mine_row + h * UNIT, UNIT), UNIT)]
            send(src.at[pl.ds(h * UNIT, UNIT)], dst, zsend.at[w], zrecv.at[w, 1, j], znext)
        dst = buf.at[pl.ds(pl.multiple_of(mine_row, 128), 128)]
        send(src, dst, ssend.at[w], srecv.at[w, 0, 0], sib)
        pltpu.make_async_copy(src, dst, lsem.at[w]).start()

    first_y(0)
    first_z(0)

    def load_chunks(src, dst, sem):
        def body(k, _):
            col = pl.multiple_of((k // 2) * LAYER + lax.rem(k, 2) * 128, 128)
            for yy in range(2):
                pltpu.make_async_copy(
                    src.at[:, pl.ds(col + yy * 256, 128)], dst.at[k, :, pl.ds(yy * 128, 128)], sem
                ).start()
            return 0

        lax.fori_loop(0, CHUNKS, body, 0)

    ins = ((uf_hbm, uf), (gs_hbm, gs), (us_hbm, us), (gf_hbm, gf))
    for src, dst in ((adt_hbm, adt), (au_hbm, au)):
        load_chunks(src, dst, ad_sem)
    for i, (src, dst) in enumerate(ins):
        load_chunks(src, dst, in_sem.at[i])

    def own_layer(s):
        return lax.rem(jnp.where(c == 0, z + NZ - s, z + s), NZ)

    def sib_layer(s):
        return lax.rem(jnp.where(c == 0, z + s, z + NZ - s), NZ)

    def rows_at(layer, group, offset, count):
        return pl.ds(pl.multiple_of(layer * LAYER + group * GROUP + offset, UNIT), count)

    def poll(w, s):
        first_step = isinstance(s, int) and s == 0
        buf = weights[w][1]
        layer = own_layer(s)
        for j, offset in enumerate((y * 128 + UNIT, y * 128, (1 - y) * 128)):
            if first_step and j < 2:
                continue
            region = buf.at[rows_at(layer, c, offset, UNIT)]
            wait_bytes(region, yfirst.at[w] if first_step else zrecv.at[w, s, j])

            @pl.when(s < NZ - 1)
            def _():
                send(region, region, zsend.at[w], zrecv.at[w, s + 1, j], znext)

            if j == 0:
                send(region, region, ysend.at[w], yrecv.at[w, s], ypal)
            if j == 1:
                both = buf.at[rows_at(layer, c, y * 128, 128)]
                send(both, both, ssend.at[w], srecv.at[w, s, 0], sib)

    def late(w, s):
        buf = weights[w][1]
        layer = own_layer(s)
        wait_bytes(buf.at[rows_at(layer, c, (1 - y) * 128 + UNIT, UNIT)], yrecv.at[w, s])
        region = buf.at[rows_at(layer, c, (1 - y) * 128, 128)]
        send(region, region, ssend.at[w], srecv.at[w, s, 1], sib)

    def ready(w, s):
        for i, yy in ((0, y), (1, 1 - y)):
            wait_bytes(weights[w][1].at[rows_at(sib_layer(s), 1 - c, yy * 128, 128)], srecv.at[w, s, i])

    def product_step(w, s, left, acc):
        buf = weights[w][1]
        own, other = own_layer(s), sib_layer(s)
        own_rows, other_rows = rows_at(own, c, 0, GROUP), rows_at(other, 1 - c, 0, GROUP)
        a, b = left[own * 2 + c], left[other * 2 + 1 - c]
        for lo, n in HCUTS:
            acc[:, lo:lo + n] += dot(a, buf[own_rows, lo:lo + n]) + dot(b, buf[other_rows, lo:lo + n])

    def hidden_step(s):
        ready(0, s)
        product_step(0, s, norm, hp)

    def frozen_block(layer, group):
        k = layer * 2 + group
        fs[k] = dot_nt(act[...], dn[rows_at(layer, group, 0, GROUP), :]).astype(BF16)
        to_x = lax.rem(layer, 4)
        shift = lax.rem(to_x + 4 - x, 4)

        @pl.when(shift != 0)
        def _():
            send(fs.at[k], fr.at[shift - 1, layer // 4, group], fsend, frecv, (dp, row_m + to_x))

    def down_step(s):
        ready(1, s)
        product_step(1, s, gf, ag)
        frozen_block(own_layer(s), c)
        frozen_block(sib_layer(s), 1 - c)

    def adapter_in():
        wait_bytes(adt, ad_sem)
        wait_bytes(au, ad_sem)
        wait_bytes(uf, in_sem.at[0])
        wait_bytes(gs, in_sem.at[1])
        pre[...] = jnp.zeros_like(pre)
        sl[...] = jnp.zeros_like(sl)

        def body(k, _):
            pre[...] += dot_nt(uf[k], adt[k])
            sl[...] += dot_nt(gs[k], au[k])
            return 0

        lax.fori_loop(0, CHUNKS, body, 0)
        v = pre[...]
        s = sigmoid(v)
        pre[...] = v * s
        sl[...] = sl[...] * (s * (1.0 + v * (1.0 - s)))
        wait_bytes(us, in_sem.at[2])
        wait_bytes(gf, in_sem.at[3])
        ssq[...] = jnp.zeros_like(ssq)

    def adapter_out(lo, hi):
        squashed = pre[...].astype(BF16)
        slope_in = sl[...].astype(BF16)

        def body(k, _):
            lower = (us[k].astype(F32) - dot(squashed, au[k])).astype(BF16)
            us[k] = lower
            value = lower.astype(F32)
            square = value * value
            ssq[...] += square[:, :128] + square[:, 128:]
            gf[k] = (gf[k].astype(F32) + dot(slope_in, adt[k])).astype(BF16)
            return 0

        lax.fori_loop(lo, hi, body, 0)

    def normalise():
        mean = jnp.sum(ssq[...], axis=1, keepdims=True) * (1.0 / D)
        invb[...] = jnp.broadcast_to(lax.rsqrt(mean + 1e-05), (T, 128))

        def body(k, _):
            scale = invb[...]
            both = jnp.concatenate([scale, scale], axis=1)
            norm[k] = (us[k].astype(F32) * both * gain_ref[k]).astype(BF16)
            return 0

        lax.fori_loop(0, CHUNKS, body, 0)
        hp[...] = jnp.zeros_like(hp)
        ag[...] = jnp.zeros_like(ag)

    def grads_1():
        both = jnp.concatenate([sl[...], pre[...]], axis=1)
        turned = both.T.astype(BF16)
        for half, (rows, right) in enumerate(((turned[:R], uf), (turned[R:], gs))):
            for q in range(2):
                part = dot(rows, right[2 * m + q])
                for yy in range(2):
                    for t in range(4):
                        lo = yy * 32 + t * 8
                        grad[half, yy, 2 * t + q] = part[lo:lo + 8]
        send(grad.at[1 - c], gr1, gsend.at[0], grecv.at[0], sib)

    def grads_2():
        wait_bytes(gr1, grecv.at[0])
        grad[c] = grad[c] + gr1[...]
        send(grad.at[c, 1 - y], gr2, gsend.at[1], grecv.at[1], ypal)

    def grads_3():
        wait_bytes(gr2, grecv.at[1])
        grad[c, y] = grad[c, y] + gr2[...]
        for k in range(1, NZ):
            send(grad.at[c, y, zshift[k]], gr3.at[k - 1], gsend.at[2], grecv.at[2], zdev[k])

    def grads_4():
        wait_bytes(gr3, grecv.at[2])
        total = grad[c, y, z]
        for k in range(NZ - 1):
            total = total + gr3[k]
        gfin[c, y, z] = total * GRAD_SCALE
        for k in range(1, NZ):
            send(gfin.at[c, y, z], gfin.at[c, y, z], gsend.at[3], grecv.at[3], zdev[k])

    def grads_5():
        wait_bytes(gr3, grecv.at[3])
        send(gfin.at[c, y], gfin.at[c, y], gsend.at[4], grecv.at[4], ypal)

    def grads_6():
        wait_bytes(gr2, grecv.at[4])
        send(gfin.at[c], gfin.at[c], gsend.at[5], grecv.at[5], sib)

    def grads_7():
        wait_bytes(gr1, grecv.at[5])
        for half, out in enumerate((o_dg, o_ug)):
            for yy in range(2):
                for t in range(4):
                    for q in range(2):
                        lo = yy * 32 + t * 8
                        piece = gfin[half, yy, 2 * t + q]
                        out[lo:lo + 8, q * 128:q * 128 + 128] = piece[:, :128]
                        out[lo:lo + 8, q * 128 + 256:q * 128 + 384] = piece[:, 128:]

    def activations():
        def body(i, _):
            rows = pl.ds(pl.multiple_of(i * 32, 32), 32)
            v = hp[rows, :]
            s = sigmoid(v)
            act[rows, :] = (v * s).astype(BF16)
            slope[rows, :] = s * (1.0 + v * (1.0 - s))
            return 0

        lax.fori_loop(0, 8, body, 0)

    def slices_out():
        for q in range(2):
            for yy in range(2):
                lo, src = q * 128 + yy * 256, slice(yy * 128, yy * 128 + 128)
                o_ls[:, lo:lo + 128] = us[2 * m + q, :, src]
                o_igf[:, lo:lo + 128] = (0.5 * gf[2 * m + q, :, src].astype(F32)).astype(BF16)

    poll(0, 0)
    adapter_in()
    late(0, 0)
    poll(0, 1)
    adapter_out(0, CHUNKS // 2)
    late(0, 1)
    poll(0, 2)
    adapter_out(CHUNKS // 2, CHUNKS)
    late(0, 2)
    normalise()

    def up_body(s, _):
        poll(0, s)
        late(0, s - 1)

        @pl.when(s == 4)
        def _():
            first_y(1)
            grads_1()

        @pl.when(s == 5)
        def _():
            grads_2()

        @pl.when(s == 6)
        def _():
            first_z(1)
            grads_3()

        hidden_step(s - 3)
        return 0

    late_done = 3
    poll(0, 3)
    wait_bytes(up.at[pl.ds(0, 128)], lsem.at[0])
    hidden_step(0)
    lax.fori_loop(late_done + 1, NZ, up_body, 0)
    poll(1, 0)
    hidden_step(5)
    late(0, 7)
    hidden_step(6)
    late(1, 0)
    poll(1, 1)
    wait_bytes(dn.at[pl.ds(0, 128)], lsem.at[1])
    hidden_step(7)
    activations()

    def down_body(s, _):
        poll(1, s)
        late(1, s - 1)

        @pl.when(s == 2)
        def _():
            grads_4()

        @pl.when(s == 3)
        def _():
            grads_5()

        @pl.when(s == 4)
        def _():
            grads_6()

        @pl.when(s == 5)
        def _():
            grads_7()
            slices_out()

        down_step(s - 2)
        return 0

    lax.fori_loop(2, NZ, down_body, 0)
    late(1, 7)
    down_step(6)
    down_step(7)

    def pre_grads(i, _):
        rows = pl.ds(pl.multiple_of(i * 32, 32), 32)
        g = (ag[rows, :] * slope[rows, :]).astype(BF16)
        pg[rows, :] = g
        part = jnp.sum(hp[rows, :] * g.astype(F32), axis=1, keepdims=True)
        stat[rows, :] = jnp.broadcast_to(part, (32, 128))
        return 0

    lax.fori_loop(0, 8, pre_grads, 0)
    mine = pl.ds(pl.multiple_of(m * SHARE, SHARE), SHARE)
    for k in range(1, NM):
        theirs = pl.ds(pl.multiple_of(mshift[k] * SHARE, SHARE), SHARE)
        send(stat.at[theirs], sr.at[k - 1], tsend, trecv, mdev[k])

    def normed_block(b, _):
        for q in range(2):
            rows = pl.ds(pl.multiple_of(b * LAYER + q * GROUP, GROUP), GROUP)
            ns[b, :, q * GROUP:q * GROUP + GROUP] = dot_nt(pg[...], up[rows, :]).astype(BF16)
        for k in range(1, NM):
            theirs = pl.ds(pl.multiple_of(mshift[k] * SHARE, SHARE), SHARE)
            send(ns.at[b, theirs], nr.at[b, k - 1], nsend, nrecv.at[b], mdev[k])
        return 0

    lax.fori_loop(0, NZ, normed_block, 0)

    wait_bytes(fr, frecv)
    far = 4 - row_m + x

    def row_sum(q, half, layer, rows):
        total = fs[2 * layer + q, rows, :].astype(F32)
        for k in range(3):
            total = total + fr[k, half, q, rows, :].astype(F32)
        return total

    for q in range(2):
        def far_half(i, _):
            rows = pl.ds(pl.multiple_of(i * 32, 32), 32)
            f2s[q, rows, :] = row_sum(q, far // 4, far, rows).astype(BF16)
            return 0

        lax.fori_loop(0, 8, far_half, 0)
    send(f2s, fr2, f2sem.at[0], f2sem.at[1], (dp, far))

    wait_bytes(sr, trecv)
    inv32 = invb[mine, :]
    total = stat[mine, :]
    for k in range(NM - 1):
        total = total + sr[k]
    curv[...] = inv32 * inv32 * total * (1.0 / D)

    def finish(b, _):
        wait_bytes(nr.at[b], nrecv.at[b])
        inv = invb[mine, :]
        inv = jnp.concatenate([inv, inv], axis=1)
        cv = jnp.concatenate([curv[...], curv[...]], axis=1)
        for q in range(2):
            lo = q * GROUP
            k2 = 2 * b + q
            normed_grad = ns[b, mine, lo:lo + GROUP].astype(F32)
            for k in range(NM - 1):
                normed_grad = normed_grad + nr[b, k, :, lo:lo + GROUP].astype(F32)
            value = (
                gs[k2, mine, :].astype(F32)
                + inv * gain_ref[k2] * normed_grad
                - us[k2, mine, :].astype(F32) * cv
            ).astype(BF16)
            outc[b, :, q * 128:q * 128 + 128] = value[:, :128]
            outc[b, :, q * 128 + 256:q * 128 + 384] = value[:, 128:]
        place = o_igs.at[mine, pl.ds(pl.multiple_of(b * LAYER, LAYER), LAYER)]
        for k in range(1, NM):
            send(outc.at[b], place, osend, orecv, mdev[k])
        pltpu.make_async_copy(outc.at[b], place, osem).start()
        return 0

    lax.fori_loop(0, NZ, finish, 0)

    wait_bytes(fr2, f2sem.at[1])
    for q in range(2):
        def rebuild(i, _):
            rows = pl.ds(pl.multiple_of(i * 32, 32), 32)
            total = row_sum(q, m // 4, m, rows) + fr2[q, rows, :].astype(F32)
            value = ((uf[2 * m + q, rows, :].astype(F32) - total) * 2.0).astype(BF16)
            for yy in range(2):
                lo = q * 128 + yy * 256
                o_lf[rows, lo:lo + 128] = value[:, yy * 128:yy * 128 + 128]
            return 0

        lax.fori_loop(0, 8, rebuild, 0)

    seven = ns.at[:, pl.ds(0, T - SHARE)]
    for w in range(2):
        buf = weights[w][1]
        wait_bytes(buf.at[pl.ds(0, 7 * CARRY * UNIT)], zsend.at[w])
        wait_bytes(buf.at[pl.ds(0, 9 * UNIT)], ysend.at[w])
        wait_bytes(buf.at[pl.ds(0, 8 * GROUP)], ssend.at[w])
    wait_bytes(fr, fsend)
    wait_bytes(f2s, f2sem.at[0])
    wait_bytes(sr, tsend)
    wait_bytes(gr1, gsend.at[0])
    wait_bytes(gr2, gsend.at[1])
    wait_bytes(gr3, gsend.at[2])
    wait_bytes(gr3, gsend.at[3])
    wait_bytes(gr2, gsend.at[4])
    wait_bytes(gr1, gsend.at[5])
    wait_bytes(seven, nsend)
    wait_bytes(seven, osend)
    wait_bytes(outc, osem)
    wait_bytes(seven, orecv)


def publish(*refs):
    ins, outs, bufs, sem = refs[:6], refs[6:12], refs[12:18], refs[18]
    order = (3, 0, 1, 2, 4, 5)
    for i in order:
        pltpu.make_async_copy(ins[i], bufs[i], sem.at[i, 0]).start()
    for i in order:
        pltpu.make_async_copy(ins[i], bufs[i], sem.at[i, 0]).wait()
        pltpu.make_async_copy(bufs[i], outs[i], sem.at[i, 1]).start()
    for i in order:
        pltpu.make_async_copy(bufs[i], outs[i], sem.at[i, 1]).wait()


def on_device(uf, us, gf, gs, gain, upw, dnw, ad, au):
    any_spec = pl.BlockSpec(memory_space=pl.ANY)
    vmem = pl.BlockSpec(memory_space=pltpu.VMEM)
    sds = jax.ShapeDtypeStruct
    gain3 = gain.astype(F32).reshape(NZ, 2, 2, 128).swapaxes(1, 2).reshape(CHUNKS, 1, GROUP)
    dma = pltpu.SemaphoreType.DMA
    chunked = pltpu.VMEM((CHUNKS, T, GROUP), BF16)
    outs = pl.pallas_call(
        kernel,
        out_shape=(
            sds((T, 512), BF16), sds((T, 512), BF16), sds((T, 512), BF16), sds((T, D), BF16),
            sds((R, 512), F32), sds((R, 512), F32),
        ),
        in_specs=[any_spec] * 4 + [vmem] + [any_spec] * 4,
        out_specs=(vmem, vmem, vmem, any_spec, vmem, vmem),
        scratch_shapes=[
            chunked, chunked, chunked, chunked, chunked,
            pltpu.VMEM((CHUNKS, R, GROUP), BF16), pltpu.VMEM((CHUNKS, R, GROUP), BF16),
            pltpu.VMEM((D, H), BF16), pltpu.VMEM((D, H), BF16),
            pltpu.VMEM((T, H), F32), pltpu.VMEM((T, H), F32), pltpu.VMEM((T, H), F32),
            pltpu.VMEM((T, H), BF16), pltpu.VMEM((T, H), BF16),
            chunked, pltpu.VMEM((3, 2, 2, T, GROUP), BF16),
            pltpu.VMEM((2, T, GROUP), BF16), pltpu.VMEM((2, T, GROUP), BF16),
            pltpu.VMEM((NZ, T, LAYER), BF16), pltpu.VMEM((NZ, NM - 1, SHARE, LAYER), BF16),
            pltpu.VMEM((NZ, SHARE, LAYER), BF16),
            pltpu.VMEM((T, R), F32), pltpu.VMEM((T, R), F32), pltpu.VMEM((T, 128), F32),
            pltpu.VMEM((T, 128), F32), pltpu.VMEM((SHARE, 128), F32), pltpu.VMEM((T, 128), F32),
            pltpu.VMEM((NM - 1, SHARE, 128), F32),
            pltpu.VMEM((2, 2, 8, 8, 256), F32), pltpu.VMEM((2, 8, 8, 256), F32),
            pltpu.VMEM((8, 8, 256), F32), pltpu.VMEM((7, 8, 256), F32),
            pltpu.VMEM((2, 2, 8, 8, 256), F32),
            dma((4,)), dma, dma((2,)), dma((2,)), dma((2, 8, 3)), dma((2,)), dma((2, 8)), dma((2,)),
            dma((2, 8, 2)), dma((2,)),
            dma, dma, dma((2,)), dma, dma((8,)), dma, dma, dma((6,)), dma((6,)), dma, dma, dma,
        ],
        compiler_params=pltpu.CompilerParams(
            collective_id=0, has_side_effects=True, vmem_limit_bytes=67000000
        ),
        name="coupling",
    )(uf, us, gf, gs, gain3, upw, dnw, ad.T, au)
    lf, ls, igf, igs, dgt, ug = pl.pallas_call(
        publish,
        out_shape=tuple(sds(o.shape, o.dtype) for o in outs),
        in_specs=[any_spec] * 6,
        out_specs=(any_spec,) * 6,
        scratch_shapes=[pltpu.VMEM(o.shape, o.dtype) for o in outs] + [dma((6, 2))],
        name="publish",
    )(*outs)
    return lf, ls, igf, igs, dgt.T, ug


def solution(mesh):
    return jax.shard_map(
        on_device,
        mesh=mesh,
        in_specs=(
            P("dp", None), P("dp", None), P("dp", None), P("dp", None), P(),
            P("dp", "mp"), P("dp", "mp"), P(), P(),
        ),
        out_specs=(
            P("dp", "mp"), P("dp", "mp"), P("dp", "mp"), P("dp", None), P("mp", None), P(None, "mp"),
        ),
        check_vma=False,
    )
```
